32 devices in a mesh: loop: 4 (over y, x), bulk: 8 (over z, core).
Axes of the slice: x: 2, y: 2, z: 4, core: 2. Of those that a mesh axis runs over, the one named last changes fastest.
Arguments:
- series: float32 [4224, 3072], P('loop', 'bulk'), may hold values from -64 to 64
Outputs:
- correlation: float32 [4, 1056, 4224], P(None, 'bulk', 'loop')
The draws below stay inside these ranges and needn't reach their ends.
All inputs are finite; a program needn't handle non-finite values.
Results may differ from the reference program's by a relative error of at most 0.0011.
Values may be sent and summed in bfloat16 or wider, within the bound.
A program may use at most 64 MiB of HBM per device.

```python
import jax
import jax.numpy as jnp
from jax import lax

ROWS_DEV = 1056
TIME = 3072
GRAY = 4224
N_LOOP = 4


def draw_series(key, part):
    keys = jax.random.split(key, 3)
    position = (jnp.arange(TIME, dtype=jnp.float32) + 0.5) / TIME
    ramp = (0.5 + position)[None, :]
    drift = jax.random.truncated_normal(keys[1], -3.0, 3.0, (GRAY, 1), jnp.float32)
    scale_row = jnp.exp(jax.random.uniform(keys[0], (GRAY, 1), jnp.float32, 0.0, jnp.log(10.0)))
    noise = jax.random.truncated_normal(keys[2], -4.0, 4.0, (GRAY, TIME), jnp.float32)
    values = scale_row * (drift * ramp + jnp.sqrt(ramp) * noise)
    return jnp.clip(values, -64.0, 64.0)


def setup_inputs(seed: int = 0) -> dict:
    key_of = jax.random.split(jax.random.key(seed), 2)
    series = draw_series(jax.random.fold_in(key_of[1], 71), 0)
    return dict(series=series)


epsilon = 1e-06

def reference(series):
    average = lax.optimization_barrier(jnp.sum(series, axis=1, keepdims=True)) / TIME
    centered = series - average
    variance = lax.optimization_barrier(jnp.sum(centered * centered, axis=1, keepdims=True)) / TIME
    zscore = (centered * lax.rsqrt(variance + epsilon)).astype(jnp.bfloat16)
    gray_blocks = zscore.reshape(N_LOOP, ROWS_DEV, TIME)

    def block_product(gray_block):
        product = lax.dot_general(gray_block, zscore, (((1,), (1,)), ((), ())), preferred_element_type=jnp.float32)
        return product / TIME
    return lax.map(block_product, gray_blocks)
```

```python
import functools
import jax
import jax.numpy as jnp
from jax import lax
from jax.experimental import pallas as pl
from jax.experimental.pallas import tpu as pltpu
from jax.sharding import PartitionSpec as P

epsilon = 1e-06
MESH = pl.DeviceIdType.MESH
NT = (((1,), (1,)), ((), ()))
TN = (((0,), (0,)), ((), ()))


def up_to(value, unit):
    return -(-value // unit) * unit


def largest_tile(rows, limit):
    return max(t for t in range(16, limit + 1, 16) if rows % t == 0)


def kernel(L, B, PIECES, x_ref, o_ref, zbuf, shr, acc, cols, stats,
           z_recv, up_send, down_send, mate_send, shr_recv, shr_send, st_recv, st_send):
    R, T = x_ref.shape
    total = T * B
    Q = B // 2
    share = R // B
    SP = shr.shape[2]
    W = min(up_to(share + 15, 16), R)
    PR = R // PIECES
    tile = largest_tile(R, 128)
    l, b = lax.axis_index("loop"), lax.axis_index("bulk")
    q, c = b // 2, b % 2
    mate = q * 2 + (1 - c)

    barrier = pltpu.get_barrier_semaphore()
    for d in range(1, B):
        pl.semaphore_signal(barrier, inc=1, device_id=(l, lax.rem(b + d, B)), device_id_type=MESH)
    for d in range(1, L):
        pl.semaphore_signal(barrier, inc=1, device_id=(lax.rem(l + d, L), b), device_id_type=MESH)

    lane = lax.broadcasted_iota(jnp.int32, (tile, 128), 1)

    @pl.loop(0, R // tile)
    def _(i):
        rows = pl.ds(pl.multiple_of(i * tile, tile), tile)
        v = x_ref[rows, :]
        mean = jnp.sum(v, axis=1, keepdims=True) / T
        dev = v - mean
        m2 = jnp.sum(dev * dev, axis=1, keepdims=True)
        cols[rows, :] = jnp.where(lane == 0, mean, jnp.where(lane == 1, m2, 0.0))

    pick = (lax.broadcasted_iota(jnp.int32, (8, 128), 0)
            == lax.broadcasted_iota(jnp.int32, (8, 128), 1)).astype(jnp.float32)
    line = lax.dot_general(pick, cols[...], NT, precision=lax.Precision.HIGHEST,
                           preferred_element_type=jnp.float32)
    stats[b] = line[:2]

    pl.semaphore_wait(barrier, B - 1 + L - 1)

    def stat_copy(source, peer):
        return pltpu.make_async_remote_copy(
            src_ref=stats.at[source], dst_ref=stats.at[source],
            send_sem=st_send.at[peer], recv_sem=st_recv.at[source],
            device_id=(l, peer), device_id_type=MESH)

    for d in range(1, B):
        stat_copy(b, lax.rem(b + d, B)).start()
    for d in range(1, B):
        other = lax.rem(b + d, B)
        stat_copy(other, other).wait_recv()

    mean = stats[0, 0:1]
    for k in range(1, B):
        mean = mean + stats[k, 0:1]
    mean = mean / B
    square = jnp.zeros_like(mean)
    for k in range(B):
        shift = stats[k, 0:1] - mean
        square = square + (stats[k, 1:2] + T * (shift * shift))
    scale = lax.rsqrt(square / total + epsilon)
    sub = lax.broadcasted_iota(jnp.int32, (8, R), 0)
    both = jnp.where(sub == 0, mean, jnp.where(sub == 1, scale, 0.0))
    cols[...] = lax.dot_general(both, pick, TN, precision=lax.Precision.HIGHEST,
                                preferred_element_type=jnp.float32)

    @pl.loop(0, R // tile)
    def _(i):
        rows = pl.ds(pl.multiple_of(i * tile, tile), tile)
        z = (x_ref[rows, :] - cols[rows, 0:1]) * cols[rows, 1:2]
        zbuf[b, rows, :] = z.astype(jnp.bfloat16)

    def piece_copy(k, piece, send_sem, peer):
        part = zbuf.at[k, pl.ds(pl.multiple_of(piece * PR, 16), PR), :]
        return pltpu.make_async_remote_copy(
            src_ref=part, dst_ref=part, send_sem=send_sem.at[k, piece],
            recv_sem=z_recv.at[k, piece], device_id=(l, peer), device_id_type=MESH)

    def share_copy(k, block, peer):
        return pltpu.make_async_remote_copy(
            src_ref=shr.at[k, block], dst_ref=shr.at[k, block], send_sem=shr_send.at[k, peer],
            recv_sem=shr_recv.at[k, block], device_id=(peer, b), device_id_type=MESH)

    has_up, has_down = q + 1 < Q, q >= 1
    start = b * share
    first = pl.multiple_of(jnp.minimum(start // 16 * 16, R - W), 16)
    need_below = PIECES - 1 - first // PR
    need_above = (first + W - 1) // PR

    def extract(k):
        window = zbuf[k, pl.ds(first, W), :]
        hot = (lax.broadcasted_iota(jnp.int32, (SP, W), 1)
               == lax.broadcasted_iota(jnp.int32, (SP, W), 0) + (start - first))
        inside = lax.broadcasted_iota(jnp.int32, (SP, W), 0) < share
        hot = jnp.where(hot & inside, 1.0, 0.0).astype(jnp.bfloat16)
        rows = lax.dot_general(hot, window, (((1,), (0,)), ((), ())),
                               preferred_element_type=jnp.float32)
        shr[k, l] = rows.astype(jnp.bfloat16)
        for d in range(1, L):
            share_copy(k, l, lax.rem(l + d, L)).start()

    def multiply(k):
        for d in range(1, L):
            other = lax.rem(l + d, L)
            share_copy(k, other, other).wait_recv()
        a = shr[k].reshape(L * SP, T)
        acc[...] += lax.dot_general(a, zbuf[k], NT, preferred_element_type=jnp.float32)

    def multiply_step(s):
        @pl.loop(0, 4)
        def _(n):
            sign = 1 - 2 * (n // 2)
            place = q - sign * s
            k = place * 2 + n % 2

            @pl.when((place >= 0) & (place < Q) & ((s > 0) | (n < 2)))
            def _():
                multiply(k)

    @pl.loop(0, PIECES)
    def _(i):
        @pl.when(has_up)
        def _():
            piece_copy(b, PIECES - 1 - i, up_send, b + 2).start()

        @pl.when(has_down)
        def _():
            piece_copy(b, i, down_send, b - 2).start()

    @pl.loop(0, PIECES)
    def _(i):
        piece_copy(b, i, mate_send, mate).start()

    acc[...] = jnp.zeros_like(acc)
    extract(b)

    @pl.loop(0, PIECES)
    def _(i):
        piece_copy(mate, i, mate_send, mate).wait_recv()

    extract(mate)

    @pl.loop(1, Q)
    def _(s):
        below, above = b - 2 * s, b + 2 * s
        from_below, from_above = q - s >= 0, q + s < Q

        @pl.loop(0, PIECES)
        def _(i):
            down_piece = PIECES - 1 - i

            @pl.when(from_below)
            def _():
                piece_copy(below, down_piece, up_send, b).wait_recv()

                @pl.when(has_up)
                def _():
                    piece_copy(below, down_piece, up_send, b + 2).start()
                piece_copy(below, down_piece, mate_send, mate).start()

            @pl.when(from_above)
            def _():
                piece_copy(above, i, down_send, b).wait_recv()

                @pl.when(has_down)
                def _():
                    piece_copy(above, i, down_send, b - 2).start()
                piece_copy(above, i, mate_send, mate).start()

            @pl.when(from_below & (i == need_below))
            def _():
                extract(below)

            @pl.when(from_above & (i == need_above))
            def _():
                extract(above)

            @pl.when(from_below)
            def _():
                piece_copy(mate - 2 * s, down_piece, mate_send, mate).wait_recv()

                @pl.when(i == need_below)
                def _():
                    extract(mate - 2 * s)

            @pl.when(from_above)
            def _():
                piece_copy(mate + 2 * s, i, mate_send, mate).wait_recv()

                @pl.when(i == need_above)
                def _():
                    extract(mate + 2 * s)

            @pl.when(i == 0)
            def _():
                multiply_step(s - 1)

    multiply_step(Q - 1)

    for j in range(L):
        o_ref[j] = acc[j * SP:j * SP + share, :] / total

    for d in range(1, B):
        other = lax.rem(b + d, B)
        stat_copy(b, other).wait_send()

    @pl.loop(0, Q)
    def _(s):
        below, above = b - 2 * s, b + 2 * s
        from_below, from_above = q - s >= 0, q + s < Q

        @pl.loop(0, PIECES)
        def _(i):
            @pl.when(from_below & has_up)
            def _():
                piece_copy(below, i, up_send, b + 2).wait_send()

            @pl.when(from_above & has_down)
            def _():
                piece_copy(above, i, down_send, b - 2).wait_send()

            @pl.when(from_below)
            def _():
                piece_copy(below, i, mate_send, mate).wait_send()

            @pl.when(from_above & (s > 0))
            def _():
                piece_copy(above, i, mate_send, mate).wait_send()

    @pl.loop(0, B)
    def _(k):
        for d in range(1, L):
            other = lax.rem(l + d, L)
            share_copy(k, l, other).wait_send()


def solution(mesh):
    L, B = mesh.shape["loop"], mesh.shape["bulk"]

    def on_device(series):
        R, T = series.shape
        share = R // B
        SP = up_to(share, 16)
        pieces = 3
        vmem = pl.BlockSpec(memory_space=pltpu.VMEM)
        dma = pltpu.SemaphoreType.DMA
        return pl.pallas_call(
            functools.partial(kernel, L, B, pieces),
            out_shape=jax.ShapeDtypeStruct((L, share, R), jnp.float32),
            in_specs=[vmem],
            out_specs=vmem,
            scratch_shapes=[
                pltpu.VMEM((B, R, T), jnp.bfloat16),
                pltpu.VMEM((B, L, SP, T), jnp.bfloat16),
                pltpu.VMEM((L * SP, R), jnp.float32),
                pltpu.VMEM((R, 128), jnp.float32),
                pltpu.VMEM((B, 2, R), jnp.float32),
                dma((B, pieces)), dma((B, pieces)), dma((B, pieces)), dma((B, pieces)),
                dma((B, L)), dma((B, L)), dma((B,)), dma((B,)),
            ],
            compiler_params=pltpu.CompilerParams(
                collective_id=0, has_side_effects=True, vmem_limit_bytes=56 * 1024 * 1024),
        )(series)

    return jax.shard_map(
        on_device, mesh=mesh, in_specs=(P("loop", "bulk"),),
        out_specs=P(None, "bulk", "loop"), check_vma=False)
```

```python
import functools
import jax
import jax.numpy as jnp
from jax import lax
from jax.experimental import pallas as pl
from jax.experimental.pallas import tpu as pltpu
from jax.sharding import PartitionSpec as P

epsilon = 1e-06
MESH = pl.DeviceIdType.MESH
NT = (((1,), (1,)), ((), ()))
TN = (((0,), (0,)), ((), ()))


def up_to(value, unit):
    return -(-value // unit) * unit


def largest_tile(rows, limit):
    return max(t for t in range(16, limit + 1, 16) if rows % t == 0)


def kernel(L, B, PIECES, x_hbm, o_ref, zbuf, shr, acc, cols, stats, x_ref,
           z_recv, up_send, down_send, mate_send, shr_recv, shr_send, st_recv, st_send, x_sem):
    R, T = x_hbm.shape
    total = T * B
    Q = B // 2
    share = R // B
    SP = shr.shape[2]
    W = min(up_to(share + 15, 16), R)
    bounds = [up_to(R * i // PIECES, 128) for i in range(PIECES)] + [R]
    tile = largest_tile(R, 128)
    l, b = lax.axis_index("loop"), lax.axis_index("bulk")
    q, c = b // 2, b % 2
    mate = q * 2 + (1 - c)

    barrier = pltpu.get_barrier_semaphore()
    for d in range(1, B):
        pl.semaphore_signal(barrier, inc=1, device_id=(l, lax.rem(b + d, B)), device_id_type=MESH)
    for d in range(1, L):
        pl.semaphore_signal(barrier, inc=1, device_id=(lax.rem(l + d, L), b), device_id_type=MESH)

    def load(i):
        rows = pl.ds(pl.multiple_of(i * tile, tile), tile)
        return pltpu.make_async_copy(x_hbm.at[rows, :], x_ref.at[rows, :], x_sem.at[i])

    @pl.loop(0, R // tile)
    def _(i):
        load(i).start()

    lane = lax.broadcasted_iota(jnp.int32, (tile, 128), 1)

    @pl.loop(0, R // tile)
    def _(i):
        rows = pl.ds(pl.multiple_of(i * tile, tile), tile)
        load(i).wait()
        v = x_ref[rows, :]
        mean = jnp.sum(v, axis=1, keepdims=True) / T
        dev = v - mean
        m2 = jnp.sum(dev * dev, axis=1, keepdims=True)
        cols[rows, :] = jnp.where(lane == 0, mean, jnp.where(lane == 1, m2, 0.0))

    pick = (lax.broadcasted_iota(jnp.int32, (8, 128), 0)
            == lax.broadcasted_iota(jnp.int32, (8, 128), 1)).astype(jnp.float32)
    line = lax.dot_general(pick, cols[...], NT, precision=lax.Precision.HIGHEST,
                           preferred_element_type=jnp.float32)
    stats[b] = line[:2]

    pl.semaphore_wait(barrier, B - 1 + L - 1)

    def stat_copy(source, peer):
        return pltpu.make_async_remote_copy(
            src_ref=stats.at[source], dst_ref=stats.at[source],
            send_sem=st_send.at[peer], recv_sem=st_recv.at[source],
            device_id=(l, peer), device_id_type=MESH)

    for d in range(1, B):
        stat_copy(b, lax.rem(b + d, B)).start()
    for d in range(1, B):
        other = lax.rem(b + d, B)
        stat_copy(other, other).wait_recv()

    mean = stats[0, 0:1]
    for k in range(1, B):
        mean = mean + stats[k, 0:1]
    mean = mean / B
    square = jnp.zeros_like(mean)
    for k in range(B):
        shift = stats[k, 0:1] - mean
        square = square + (stats[k, 1:2] + T * (shift * shift))
    scale = lax.rsqrt(square / total + epsilon)
    sub = lax.broadcasted_iota(jnp.int32, (8, R), 0)
    both = jnp.where(sub == 0, mean, jnp.where(sub == 1, scale, 0.0))
    cols[...] = lax.dot_general(both, pick, TN, precision=lax.Precision.HIGHEST,
                                preferred_element_type=jnp.float32)

    def normalise(piece):
        size = bounds[piece + 1] - bounds[piece]
        step = largest_tile(size, 128)

        @pl.loop(0, size // step)
        def _(i):
            rows = pl.ds(pl.multiple_of(bounds[piece] + i * step, 16), step)
            z = (x_ref[rows, :] - cols[rows, 0:1]) * cols[rows, 1:2]
            zbuf[b, rows, :] = z.astype(jnp.bfloat16)

    def piece_copy(k, piece, send_sem, peer):
        part = zbuf.at[k, pl.ds(bounds[piece], bounds[piece + 1] - bounds[piece]), :]
        return pltpu.make_async_remote_copy(
            src_ref=part, dst_ref=part, send_sem=send_sem.at[k, piece],
            recv_sem=z_recv.at[k, piece], device_id=(l, peer), device_id_type=MESH)

    def share_copy(k, block, peer):
        return pltpu.make_async_remote_copy(
            src_ref=shr.at[k, block], dst_ref=shr.at[k, block], send_sem=shr_send.at[k, peer],
            recv_sem=shr_recv.at[k, block], device_id=(peer, b), device_id_type=MESH)

    has_up, has_down = q + 1 < Q, q >= 1
    start = b * share
    first = pl.multiple_of(jnp.minimum(start // 16 * 16, R - W), 16)
    need_below = PIECES - 1 - sum((first >= x).astype(jnp.int32) for x in bounds[1:-1])
    need_above = sum((first + W > x).astype(jnp.int32) for x in bounds[1:-1])

    def extract(k):
        window = zbuf[k, pl.ds(first, W), :]
        hot = (lax.broadcasted_iota(jnp.int32, (SP, W), 1)
               == lax.broadcasted_iota(jnp.int32, (SP, W), 0) + (start - first))
        inside = lax.broadcasted_iota(jnp.int32, (SP, W), 0) < share
        hot = jnp.where(hot & inside, 1.0, 0.0).astype(jnp.bfloat16)
        rows = lax.dot_general(hot, window, (((1,), (0,)), ((), ())),
                               preferred_element_type=jnp.float32)
        shr[k, l] = rows.astype(jnp.bfloat16)
        for d in range(1, L):
            share_copy(k, l, lax.rem(l + d, L)).start()

    def wait_shares(place):
        for core in range(2):
            k = place * 2 + core
            for d in range(1, L):
                other = lax.rem(l + d, L)
                share_copy(k, other, other).wait_recv()

    def multiply(place):
        part = None
        wait_shares(place)
        for core in range(2):
            k = place * 2 + core
            a = shr[k].reshape(L * SP, T)
            term = lax.dot_general(a, zbuf[k], NT, preferred_element_type=jnp.float32)
            part = term if part is None else part + term
        acc[...] += part

    def multiply_step(s):
        @pl.loop(0, 2)
        def _(n):
            place = q - (1 - 2 * n) * s

            @pl.when((place >= 0) & (place < Q) & ((s > 0) | (n < 1)))
            def _():
                multiply(place)

    done = set()

    def ready(piece):
        if piece not in done:
            done.add(piece)
            normalise(piece)

    for i in range(PIECES):
        ready(PIECES - 1 - i)

        @pl.when(has_up)
        def _():
            piece_copy(b, PIECES - 1 - i, up_send, b + 2).start()

        ready(i)

        @pl.when(has_down)
        def _():
            piece_copy(b, i, down_send, b - 2).start()

    for i in range(PIECES):
        piece_copy(b, i, mate_send, mate).start()

    acc[...] = jnp.zeros_like(acc)
    extract(b)

    for i in range(PIECES):
        piece_copy(mate, i, mate_send, mate).wait_recv()

    extract(mate)

    def arrive(s, i, between=None):
        below, above = b - 2 * s, b + 2 * s
        from_below, from_above = q - s >= 0, q + s < Q
        down_piece = PIECES - 1 - i

        @pl.when(from_below)
        def _():
            piece_copy(below, down_piece, up_send, b).wait_recv()

            @pl.when(has_up)
            def _():
                piece_copy(below, down_piece, up_send, b + 2).start()
            piece_copy(below, down_piece, mate_send, mate).start()

        @pl.when(from_above)
        def _():
            piece_copy(above, i, down_send, b).wait_recv()

            @pl.when(has_down)
            def _():
                piece_copy(above, i, down_send, b - 2).start()
            piece_copy(above, i, mate_send, mate).start()

        @pl.when(from_below & (i == need_below))
        def _():
            extract(below)

        @pl.when(from_above & (i == need_above))
        def _():
            extract(above)

        if between is not None:
            between()

        @pl.when(from_below)
        def _():
            piece_copy(mate - 2 * s, down_piece, mate_send, mate).wait_recv()

            @pl.when(i == need_below)
            def _():
                extract(mate - 2 * s)

        @pl.when(from_above)
        def _():
            piece_copy(mate + 2 * s, i, mate_send, mate).wait_recv()

            @pl.when(i == need_above)
            def _():
                extract(mate + 2 * s)

        if i == 0:
            multiply_step(s - 1)

    def finish(piece, place):
        lo, hi = bounds[piece], bounds[piece + 1]
        part = acc[:, lo:hi]
        if place is not None:
            for core in range(2):
                k = place * 2 + core
                a = shr[k].reshape(L * SP, T)
                part = part + lax.dot_general(a, zbuf[k, lo:hi, :], NT,
                                              preferred_element_type=jnp.float32)
        part = part / total
        for j in range(L):
            o_ref[:, j, lo:hi] = part[j * SP:j * SP + share]

    @pl.loop(1, Q - 1)
    def _(s):
        for i in range(PIECES):
            arrive(s, i)

    def finish_ends(steps):
        for end, place in ((Q - 1, 0), (0, Q - 1)):
            @pl.when(q == end)
            def _():
                for i in steps:
                    finish(PIECES - 1 - i if end else i, place)

    def finish_early():
        for end, place in ((Q - 1, 0), (0, Q - 1)):
            @pl.when(q == end)
            def _():
                wait_shares(place)

        finish_ends(range(PIECES - 1))

    for i in range(PIECES):
        arrive(Q - 1, i, finish_early if i == PIECES - 1 else None)
    finish_ends([PIECES - 1])

    @pl.when((q > 0) & (q < Q - 1))
    def _():
        for i in range(PIECES):
            finish(i, None)

    for d in range(1, B):
        other = lax.rem(b + d, B)
        stat_copy(b, other).wait_send()

    @pl.loop(0, Q)
    def _(s):
        below, above = b - 2 * s, b + 2 * s
        from_below, from_above = q - s >= 0, q + s < Q

        for i in range(PIECES):
            @pl.when(from_below & has_up)
            def _():
                piece_copy(below, i, up_send, b + 2).wait_send()

            @pl.when(from_above & has_down)
            def _():
                piece_copy(above, i, down_send, b - 2).wait_send()

            @pl.when(from_below)
            def _():
                piece_copy(below, i, mate_send, mate).wait_send()

            @pl.when(from_above & (s > 0))
            def _():
                piece_copy(above, i, mate_send, mate).wait_send()

    @pl.loop(0, B)
    def _(k):
        for d in range(1, L):
            other = lax.rem(l + d, L)
            share_copy(k, l, other).wait_send()


def solution(mesh):
    L, B = mesh.shape["loop"], mesh.shape["bulk"]

    def on_device(series):
        R, T = series.shape
        share = R // B
        SP = up_to(share, 16)
        pieces = 3
        vmem = pl.BlockSpec(memory_space=pltpu.VMEM)
        dma = pltpu.SemaphoreType.DMA
        return pl.pallas_call(
            functools.partial(kernel, L, B, pieces),
            out_shape=jax.ShapeDtypeStruct((share, L, R), jnp.float32),
            in_specs=[pl.BlockSpec(memory_space=pltpu.HBM)],
            out_specs=vmem,
            scratch_shapes=[
                pltpu.VMEM((B, R, T), jnp.bfloat16),
                pltpu.VMEM((B, L, SP, T), jnp.bfloat16),
                pltpu.VMEM((L * SP, R), jnp.float32),
                pltpu.VMEM((R, 128), jnp.float32),
                pltpu.VMEM((B, 2, R), jnp.float32),
                pltpu.VMEM((R, T), jnp.float32),
                dma((B, pieces)), dma((B, pieces)), dma((B, pieces)), dma((B, pieces)),
                dma((B, L)), dma((B, L)), dma((B,)), dma((B,)), dma((R // largest_tile(R, 128),)),
            ],
            compiler_params=pltpu.CompilerParams(
                collective_id=0, has_side_effects=True, vmem_limit_bytes=26 * 1024 * 1024),
        )(pltpu.with_memory_space_constraint(series, pltpu.HBM)).transpose(1, 0, 2)

    return jax.shard_map(
        on_device, mesh=mesh, in_specs=(P("loop", "bulk"),),
        out_specs=P(None, "bulk", "loop"), check_vma=False)
```

```python
import functools
import jax
import jax.numpy as jnp
from jax import lax
from jax.experimental import pallas as pl
from jax.experimental.pallas import tpu as pltpu
from jax.sharding import PartitionSpec as P

epsilon = 1e-06
MESH = pl.DeviceIdType.MESH
NT = (((1,), (1,)), ((), ()))
TN = (((0,), (0,)), ((), ()))


def up_to(value, unit):
    return -(-value // unit) * unit


def largest_tile(rows, limit):
    return max(t for t in range(16, limit + 1, 16) if rows % t == 0)


def kernel(L, B, PIECES, x_hbm, o_ref, zbuf, shr, acc, cols, stats, x_ref,
           z_recv, up_send, down_send, mate_send, shr_recv, shr_send, st_recv, st_send, x_sem):
    R, T = x_hbm.shape
    total = T * B
    Q = B // 2
    share = R // B
    SP = shr.shape[2]
    W = min(up_to(share + 15, 16), R)
    bounds = [up_to(R * i // PIECES, 128) for i in range(PIECES)] + [R]
    tile = largest_tile(R, 128)
    l, b = lax.axis_index("loop"), lax.axis_index("bulk")
    q, c = b // 2, b % 2
    mate = q * 2 + (1 - c)

    def load(i):
        rows = pl.ds(pl.multiple_of(i * tile, tile), tile)
        return pltpu.make_async_copy(x_hbm.at[rows, :], x_ref.at[rows, :], x_sem.at[i])

    @pl.loop(0, R // tile)
    def _(i):
        load(i).start()

    barrier = pltpu.get_barrier_semaphore()
    outer = (q < Q // 4) | ((q >= Q // 2) & (q < Q - Q // 4))
    sign = jnp.where(outer, -1, 1)

    def far_first(act):
        for e in range(B):
            peer = lax.rem(2 * B - 1 - b + sign * e, B)

            @pl.when(peer != b)
            def _():
                act(peer)

    for d in range(1, B):
        pl.semaphore_signal(barrier, inc=1, device_id=(l, lax.rem(b + d, B)), device_id_type=MESH)
    for d in range(1, L):
        pl.semaphore_signal(barrier, inc=1, device_id=(lax.rem(l + d, L), b), device_id_type=MESH)

    lane = lax.broadcasted_iota(jnp.int32, (tile, 128), 1)

    @pl.loop(0, R // tile)
    def _(i):
        rows = pl.ds(pl.multiple_of(i * tile, tile), tile)
        load(i).wait()
        v = x_ref[rows, :]
        mean = jnp.sum(v, axis=1, keepdims=True) / T
        dev = v - mean
        m2 = jnp.sum(dev * dev, axis=1, keepdims=True)
        cols[rows, :] = jnp.where(lane == 0, mean, jnp.where(lane == 1, m2, 0.0))

    pick = (lax.broadcasted_iota(jnp.int32, (8, 128), 0)
            == lax.broadcasted_iota(jnp.int32, (8, 128), 1)).astype(jnp.float32)
    line = lax.dot_general(pick, cols[...], NT, precision=lax.Precision.HIGHEST,
                           preferred_element_type=jnp.float32)
    stats[b] = line[:2]

    pl.semaphore_wait(barrier, B - 1 + L - 1)

    def stat_copy(source, peer):
        return pltpu.make_async_remote_copy(
            src_ref=stats.at[source], dst_ref=stats.at[source],
            send_sem=st_send.at[peer], recv_sem=st_recv.at[source],
            device_id=(l, peer), device_id_type=MESH)

    far_first(lambda peer: stat_copy(b, peer).start())
    for d in range(1, B):
        other = lax.rem(b + d, B)
        stat_copy(other, other).wait_recv()

    mean = stats[0, 0:1]
    for k in range(1, B):
        mean = mean + stats[k, 0:1]
    mean = mean / B
    square = jnp.zeros_like(mean)
    for k in range(B):
        shift = stats[k, 0:1] - mean
        square = square + (stats[k, 1:2] + T * (shift * shift))
    scale = lax.rsqrt(square / total + epsilon)
    sub = lax.broadcasted_iota(jnp.int32, (8, R), 0)
    both = jnp.where(sub == 0, mean, jnp.where(sub == 1, scale, 0.0))
    cols[...] = lax.dot_general(both, pick, TN, precision=lax.Precision.HIGHEST,
                                preferred_element_type=jnp.float32)

    def normalise(piece):
        size = bounds[piece + 1] - bounds[piece]
        step = largest_tile(size, 128)

        @pl.loop(0, size // step)
        def _(i):
            rows = pl.ds(pl.multiple_of(bounds[piece] + i * step, 16), step)
            z = (x_ref[rows, :] - cols[rows, 0:1]) * cols[rows, 1:2]
            zbuf[b, rows, :] = z.astype(jnp.bfloat16)

    def piece_copy(k, piece, send_sem, peer):
        part = zbuf.at[k, pl.ds(bounds[piece], bounds[piece + 1] - bounds[piece]), :]
        return pltpu.make_async_remote_copy(
            src_ref=part, dst_ref=part, send_sem=send_sem.at[k, piece],
            recv_sem=z_recv.at[k, piece], device_id=(l, peer), device_id_type=MESH)

    def share_copy(k, block, peer):
        return pltpu.make_async_remote_copy(
            src_ref=shr.at[k, block], dst_ref=shr.at[k, block], send_sem=shr_send.at[k, peer],
            recv_sem=shr_recv.at[k, block], device_id=(peer, b), device_id_type=MESH)

    has_up, has_down = q + 1 < Q, q >= 1
    start = b * share
    first = pl.multiple_of(jnp.minimum(start // 16 * 16, R - W), 16)
    need_below = PIECES - 1 - sum((first >= x).astype(jnp.int32) for x in bounds[1:-1])
    need_above = sum((first + W > x).astype(jnp.int32) for x in bounds[1:-1])

    def extract(k):
        window = zbuf[k, pl.ds(first, W), :]
        hot = (lax.broadcasted_iota(jnp.int32, (SP, W), 1)
               == lax.broadcasted_iota(jnp.int32, (SP, W), 0) + (start - first))
        inside = lax.broadcasted_iota(jnp.int32, (SP, W), 0) < share
        hot = jnp.where(hot & inside, 1.0, 0.0).astype(jnp.bfloat16)
        rows = lax.dot_general(hot, window, (((1,), (0,)), ((), ())),
                               preferred_element_type=jnp.float32)
        shr[k, l] = rows.astype(jnp.bfloat16)
        for d in range(1, L):
            share_copy(k, l, lax.rem(l + d, L)).start()

    def wait_shares(place):
        for core in range(2):
            k = place * 2 + core
            for d in range(1, L):
                other = lax.rem(l + d, L)
                share_copy(k, other, other).wait_recv()

    def multiply(place):
        part = None
        wait_shares(place)
        for core in range(2):
            k = place * 2 + core
            a = shr[k].reshape(L * SP, T)
            term = lax.dot_general(a, zbuf[k], NT, preferred_element_type=jnp.float32)
            part = term if part is None else part + term
        acc[...] += part

    def multiply_step(s):
        @pl.loop(0, 2)
        def _(n):
            place = q - (1 - 2 * n) * s

            @pl.when((place >= 0) & (place < Q) & ((s > 0) | (n < 1)))
            def _():
                multiply(place)

    done = set()

    def ready(piece):
        if piece not in done:
            done.add(piece)
            normalise(piece)

    for i in range(PIECES):
        ready(PIECES - 1 - i)

        @pl.when(has_up)
        def _():
            piece_copy(b, PIECES - 1 - i, up_send, b + 2).start()

        ready(i)

        @pl.when(has_down)
        def _():
            piece_copy(b, i, down_send, b - 2).start()

    for i in range(PIECES):
        piece_copy(b, i, mate_send, mate).start()

    extract(b)
    acc[...] = jnp.zeros_like(acc)

    for i in range(PIECES):
        piece_copy(mate, i, mate_send, mate).wait_recv()

    extract(mate)

    def arrive(s, i, between=None):
        below, above = b - 2 * s, b + 2 * s
        from_below, from_above = q - s >= 0, q + s < Q
        down_piece = PIECES - 1 - i

        @pl.when(from_below)
        def _():
            piece_copy(below, down_piece, up_send, b).wait_recv()

            @pl.when(has_up)
            def _():
                piece_copy(below, down_piece, up_send, b + 2).start()
            piece_copy(below, down_piece, mate_send, mate).start()

        @pl.when(from_above)
        def _():
            piece_copy(above, i, down_send, b).wait_recv()

            @pl.when(has_down)
            def _():
                piece_copy(above, i, down_send, b - 2).start()
            piece_copy(above, i, mate_send, mate).start()

        @pl.when(from_below & (i == need_below))
        def _():
            extract(below)

        @pl.when(from_above & (i == need_above))
        def _():
            extract(above)

        if between is not None:
            between()

        @pl.when(from_below)
        def _():
            piece_copy(mate - 2 * s, down_piece, mate_send, mate).wait_recv()

            @pl.when(i == need_below)
            def _():
                extract(mate - 2 * s)

        @pl.when(from_above)
        def _():
            piece_copy(mate + 2 * s, i, mate_send, mate).wait_recv()

            @pl.when(i == need_above)
            def _():
                extract(mate + 2 * s)

        if i == 0:
            multiply_step(s - 1)

    def finish(piece, place):
        lo, hi = bounds[piece], bounds[piece + 1]
        part = acc[:, lo:hi]
        if place is not None:
            for core in range(2):
                k = place * 2 + core
                a = shr[k].reshape(L * SP, T)
                part = part + lax.dot_general(a, zbuf[k, lo:hi, :], NT,
                                              preferred_element_type=jnp.float32)
        part = part * (1.0 / total)
        for j in range(L):
            o_ref[:, j, lo:hi] = part[j * SP:j * SP + share]

    @pl.loop(1, Q - 1)
    def _(s):
        for i in range(PIECES):
            arrive(s, i)

    def finish_ends(steps):
        for end, place in ((Q - 1, 0), (0, Q - 1)):
            @pl.when(q == end)
            def _():
                for i in steps:
                    finish(PIECES - 1 - i if end else i, place)

    def finish_early():
        for end, place in ((Q - 1, 0), (0, Q - 1)):
            @pl.when(q == end)
            def _():
                wait_shares(place)

        finish_ends(range(PIECES - 1))

    for i in range(PIECES):
        arrive(Q - 1, i, finish_early if i == PIECES - 1 else None)
    finish_ends([PIECES - 1])

    @pl.when((q > 0) & (q < Q - 1))
    def _():
        for i in range(PIECES):
            finish(i, None)

    for d in range(1, B):
        other = lax.rem(b + d, B)
        stat_copy(b, other).wait_send()

    @pl.loop(0, Q)
    def _(s):
        below, above = b - 2 * s, b + 2 * s
        from_below, from_above = q - s >= 0, q + s < Q

        for i in range(PIECES):
            @pl.when(from_below & has_up)
            def _():
                piece_copy(below, i, up_send, b + 2).wait_send()

            @pl.when(from_above & has_down)
            def _():
                piece_copy(above, i, down_send, b - 2).wait_send()

            @pl.when(from_below)
            def _():
                piece_copy(below, i, mate_send, mate).wait_send()

            @pl.when(from_above & (s > 0))
            def _():
                piece_copy(above, i, mate_send, mate).wait_send()

    @pl.loop(0, B)
    def _(k):
        for d in range(1, L):
            other = lax.rem(l + d, L)
            share_copy(k, l, other).wait_send()


def solution(mesh):
    L, B = mesh.shape["loop"], mesh.shape["bulk"]

    def on_device(series):
        R, T = series.shape
        share = R // B
        SP = up_to(share, 16)
        pieces = 3
        vmem = pl.BlockSpec(memory_space=pltpu.VMEM)
        dma = pltpu.SemaphoreType.DMA
        return pl.pallas_call(
            functools.partial(kernel, L, B, pieces),
            out_shape=jax.ShapeDtypeStruct((share, L, R), jnp.float32),
            in_specs=[pl.BlockSpec(memory_space=pltpu.HBM)],
            out_specs=vmem,
            scratch_shapes=[
                pltpu.VMEM((B, R, T), jnp.bfloat16),
                pltpu.VMEM((B, L, SP, T), jnp.bfloat16),
                pltpu.VMEM((L * SP, R), jnp.float32),
                pltpu.VMEM((R, 128), jnp.float32),
                pltpu.VMEM((B, 2, R), jnp.float32),
                pltpu.VMEM((R, T), jnp.float32),
                dma((B, pieces)), dma((B, pieces)), dma((B, pieces)), dma((B, pieces)),
                dma((B, L)), dma((B, L)), dma((B,)), dma((B,)), dma((R // largest_tile(R, 128),)),
            ],
            compiler_params=pltpu.CompilerParams(
                collective_id=0, has_side_effects=True, vmem_limit_bytes=26 * 1024 * 1024),
        )(pltpu.with_memory_space_constraint(series, pltpu.HBM)).transpose(1, 0, 2)

    return jax.shard_map(
        on_device, mesh=mesh, in_specs=(P("loop", "bulk"),),
        out_specs=P(None, "bulk", "loop"), check_vma=False)
```

```python
import functools
import jax
import jax.numpy as jnp
from jax import lax
from jax.experimental import pallas as pl
from jax.experimental.pallas import tpu as pltpu
from jax.sharding import PartitionSpec as P

epsilon = 1e-06
MESH = pl.DeviceIdType.MESH
NT = (((1,), (1,)), ((), ()))
TN = (((0,), (0,)), ((), ()))


def up_to(value, unit):
    return -(-value // unit) * unit


def largest_tile(rows, limit):
    return max(t for t in range(16, limit + 1, 16) if rows % t == 0)


def kernel(L, B, PIECES, x_hbm, o_ref, zbuf, shr, acc, cols, stats, x_ref,
           z_recv, up_send, down_send, mate_send, shr_recv, shr_send, st_recv, st_send, x_sem):
    R, T = x_hbm.shape
    total = T * B
    Q = B // 2
    share = R // B
    SP = shr.shape[2]
    W = min(up_to(share + 15, 16), R)
    bounds = [up_to(R * i // PIECES, 128) for i in range(PIECES)] + [R]
    tile = largest_tile(R, 128)
    l, b = lax.axis_index("loop"), lax.axis_index("bulk")
    q, c = b // 2, b % 2
    mate = q * 2 + (1 - c)

    barrier = pltpu.get_barrier_semaphore()
    for d in range(1, B):
        pl.semaphore_signal(barrier, inc=1, device_id=(l, lax.rem(b + d, B)), device_id_type=MESH)
    for d in range(1, L):
        pl.semaphore_signal(barrier, inc=1, device_id=(lax.rem(l + d, L), b), device_id_type=MESH)

    def load(i):
        rows = pl.ds(pl.multiple_of(i * tile, tile), tile)
        return pltpu.make_async_copy(x_hbm.at[rows, :], x_ref.at[rows, :], x_sem.at[i])

    @pl.loop(0, R // tile)
    def _(i):
        load(i).start()

    lane = lax.broadcasted_iota(jnp.int32, (tile, 128), 1)

    @pl.loop(0, R // tile)
    def _(i):
        rows = pl.ds(pl.multiple_of(i * tile, tile), tile)
        load(i).wait()
        v = x_ref[rows, :]
        mean = jnp.sum(v, axis=1, keepdims=True) / T
        dev = v - mean
        m2 = jnp.sum(dev * dev, axis=1, keepdims=True)
        cols[rows, :] = jnp.where(lane == 0, mean, jnp.where(lane == 1, m2, 0.0))

    pick = (lax.broadcasted_iota(jnp.int32, (8, 128), 0)
            == lax.broadcasted_iota(jnp.int32, (8, 128), 1)).astype(jnp.float32)
    line = lax.dot_general(pick, cols[...], NT, precision=lax.Precision.HIGHEST,
                           preferred_element_type=jnp.float32)
    stats[b] = line[:2]

    pl.semaphore_wait(barrier, B - 1 + L - 1)

    def stat_copy(source, peer):
        return pltpu.make_async_remote_copy(
            src_ref=stats.at[source], dst_ref=stats.at[source],
            send_sem=st_send.at[peer], recv_sem=st_recv.at[source],
            device_id=(l, peer), device_id_type=MESH)

    for d in range(1, B):
        stat_copy(b, lax.rem(b + d, B)).start()
    for d in range(1, B):
        other = lax.rem(b + d, B)
        stat_copy(other, other).wait_recv()

    mean = stats[0, 0:1]
    for k in range(1, B):
        mean = mean + stats[k, 0:1]
    mean = mean / B
    square = jnp.zeros_like(mean)
    for k in range(B):
        shift = stats[k, 0:1] - mean
        square = square + (stats[k, 1:2] + T * (shift * shift))
    scale = lax.rsqrt(square / total + epsilon)
    sub = lax.broadcasted_iota(jnp.int32, (8, R), 0)
    both = jnp.where(sub == 0, mean, jnp.where(sub == 1, scale, 0.0))
    cols[...] = lax.dot_general(both, pick, TN, precision=lax.Precision.HIGHEST,
                                preferred_element_type=jnp.float32)

    def normalise(piece):
        size = bounds[piece + 1] - bounds[piece]
        step = largest_tile(size, 128)

        @pl.loop(0, size // step)
        def _(i):
            rows = pl.ds(pl.multiple_of(bounds[piece] + i * step, 16), step)
            z = (x_ref[rows, :] - cols[rows, 0:1]) * cols[rows, 1:2]
            zbuf[b, rows, :] = z.astype(jnp.bfloat16)

    def piece_copy(k, piece, send_sem, peer):
        part = zbuf.at[k, pl.ds(bounds[piece], bounds[piece + 1] - bounds[piece]), :]
        return pltpu.make_async_remote_copy(
            src_ref=part, dst_ref=part, send_sem=send_sem.at[k, piece],
            recv_sem=z_recv.at[k, piece], device_id=(l, peer), device_id_type=MESH)

    def share_copy(k, block, peer):
        return pltpu.make_async_remote_copy(
            src_ref=shr.at[k, block], dst_ref=shr.at[k, block], send_sem=shr_send.at[k, peer],
            recv_sem=shr_recv.at[k, block], device_id=(peer, b), device_id_type=MESH)

    has_up, has_down = q + 1 < Q, q >= 1
    start = b * share
    first = pl.multiple_of(jnp.minimum(start // 16 * 16, R - W), 16)
    need_below = PIECES - 1 - sum((first >= x).astype(jnp.int32) for x in bounds[1:-1])
    need_above = sum((first + W > x).astype(jnp.int32) for x in bounds[1:-1])

    def extract(k):
        window = zbuf[k, pl.ds(first, W), :]
        hot = (lax.broadcasted_iota(jnp.int32, (SP, W), 1)
               == lax.broadcasted_iota(jnp.int32, (SP, W), 0) + (start - first))
        inside = lax.broadcasted_iota(jnp.int32, (SP, W), 0) < share
        hot = jnp.where(hot & inside, 1.0, 0.0).astype(jnp.bfloat16)
        rows = lax.dot_general(hot, window, (((1,), (0,)), ((), ())),
                               preferred_element_type=jnp.float32)
        shr[k, l] = rows.astype(jnp.bfloat16)
        for d in range(1, L):
            share_copy(k, l, lax.rem(l + d, L)).start()

    def wait_shares(place):
        for core in range(2):
            k = place * 2 + core
            for d in range(1, L):
                other = lax.rem(l + d, L)
                share_copy(k, other, other).wait_recv()

    def multiply(place):
        part = None
        wait_shares(place)
        for core in range(2):
            k = place * 2 + core
            a = shr[k].reshape(L * SP, T)
            term = lax.dot_general(a, zbuf[k], NT, preferred_element_type=jnp.float32)
            part = term if part is None else part + term
        acc[...] += part

    def multiply_step(s):
        @pl.loop(0, 2)
        def _(n):
            place = q - (1 - 2 * n) * s

            @pl.when((place >= 0) & (place < Q) & ((s > 0) | (n < 1)))
            def _():
                multiply(place)

    def send_own(up_first):
        done = set()

        def send(up, i):
            piece = PIECES - 1 - i if up else i
            if piece not in done:
                done.add(piece)
                normalise(piece)

            @pl.when(has_up if up else has_down)
            def _():
                if up:
                    piece_copy(b, piece, up_send, b + 2).start()
                else:
                    piece_copy(b, piece, down_send, b - 2).start()

        for i in range(PIECES):
            send(up_first, i)
            send(not up_first, i)

    @pl.when(q >= Q // 2)
    def _():
        send_own(True)

    @pl.when(q < Q // 2)
    def _():
        send_own(False)

    for i in range(PIECES):
        piece_copy(b, i, mate_send, mate).start()

    acc[...] = jnp.zeros_like(acc)
    extract(b)

    for i in range(PIECES):
        piece_copy(mate, i, mate_send, mate).wait_recv()

    extract(mate)

    def arrive(s, i, between=None):
        below, above = b - 2 * s, b + 2 * s
        from_below, from_above = q - s >= 0, q + s < Q
        down_piece = PIECES - 1 - i

        @pl.when(from_below)
        def _():
            piece_copy(below, down_piece, up_send, b).wait_recv()

            @pl.when(has_up)
            def _():
                piece_copy(below, down_piece, up_send, b + 2).start()
            piece_copy(below, down_piece, mate_send, mate).start()

        @pl.when(from_above)
        def _():
            piece_copy(above, i, down_send, b).wait_recv()

            @pl.when(has_down)
            def _():
                piece_copy(above, i, down_send, b - 2).start()
            piece_copy(above, i, mate_send, mate).start()

        @pl.when(from_below & (i == need_below))
        def _():
            extract(below)

        @pl.when(from_above & (i == need_above))
        def _():
            extract(above)

        if between is not None:
            between()

        @pl.when(from_below)
        def _():
            piece_copy(mate - 2 * s, down_piece, mate_send, mate).wait_recv()

            @pl.when(i == need_below)
            def _():
                extract(mate - 2 * s)

        @pl.when(from_above)
        def _():
            piece_copy(mate + 2 * s, i, mate_send, mate).wait_recv()

            @pl.when(i == need_above)
            def _():
                extract(mate + 2 * s)

        if i == 0:
            multiply_step(s - 1)

    def finish(piece, place):
        lo, hi = bounds[piece], bounds[piece + 1]
        part = acc[:, lo:hi]
        if place is not None:
            for core in range(2):
                k = place * 2 + core
                a = shr[k].reshape(L * SP, T)
                part = part + lax.dot_general(a, zbuf[k, lo:hi, :], NT,
                                              preferred_element_type=jnp.float32)
        part = part / total
        for j in range(L):
            o_ref[:, j, lo:hi] = part[j * SP:j * SP + share]

    @pl.loop(1, Q - 1)
    def _(s):
        for i in range(PIECES):
            arrive(s, i)

    def finish_ends(steps):
        for end, place in ((Q - 1, 0), (0, Q - 1)):
            @pl.when(q == end)
            def _():
                for i in steps:
                    finish(PIECES - 1 - i if end else i, place)

    def finish_early():
        for end, place in ((Q - 1, 0), (0, Q - 1)):
            @pl.when(q == end)
            def _():
                wait_shares(place)

        finish_ends(range(PIECES - 1))

    for i in range(PIECES):
        arrive(Q - 1, i, finish_early if i == PIECES - 1 else None)
    finish_ends([PIECES - 1])

    @pl.when((q > 0) & (q < Q - 1))
    def _():
        for i in range(PIECES):
            finish(i, None)

    for d in range(1, B):
        other = lax.rem(b + d, B)
        stat_copy(b, other).wait_send()

    @pl.loop(0, Q)
    def _(s):
        below, above = b - 2 * s, b + 2 * s
        from_below, from_above = q - s >= 0, q + s < Q

        for i in range(PIECES):
            @pl.when(from_below & has_up)
            def _():
                piece_copy(below, i, up_send, b + 2).wait_send()

            @pl.when(from_above & has_down)
            def _():
                piece_copy(above, i, down_send, b - 2).wait_send()

            @pl.when(from_below)
            def _():
                piece_copy(below, i, mate_send, mate).wait_send()

            @pl.when(from_above & (s > 0))
            def _():
                piece_copy(above, i, mate_send, mate).wait_send()

    @pl.loop(0, B)
    def _(k):
        for d in range(1, L):
            other = lax.rem(l + d, L)
            share_copy(k, l, other).wait_send()


def solution(mesh):
    L, B = mesh.shape["loop"], mesh.shape["bulk"]

    def on_device(series):
        R, T = series.shape
        share = R // B
        SP = up_to(share, 16)
        pieces = 3
        vmem = pl.BlockSpec(memory_space=pltpu.VMEM)
        dma = pltpu.SemaphoreType.DMA
        return pl.pallas_call(
            functools.partial(kernel, L, B, pieces),
            out_shape=jax.ShapeDtypeStruct((share, L, R), jnp.float32),
            in_specs=[pl.BlockSpec(memory_space=pltpu.HBM)],
            out_specs=vmem,
            scratch_shapes=[
                pltpu.VMEM((B, R, T), jnp.bfloat16),
                pltpu.VMEM((B, L, SP, T), jnp.bfloat16),
                pltpu.VMEM((L * SP, R), jnp.float32),
                pltpu.VMEM((R, 128), jnp.float32),
                pltpu.VMEM((B, 2, R), jnp.float32),
                pltpu.VMEM((R, T), jnp.float32),
                dma((B, pieces)), dma((B, pieces)), dma((B, pieces)), dma((B, pieces)),
                dma((B, L)), dma((B, L)), dma((B,)), dma((B,)), dma((R // largest_tile(R, 128),)),
            ],
            compiler_params=pltpu.CompilerParams(
                collective_id=0, has_side_effects=True, vmem_limit_bytes=26 * 1024 * 1024),
        )(pltpu.with_memory_space_constraint(series, pltpu.HBM)).transpose(1, 0, 2)

    return jax.shard_map(
        on_device, mesh=mesh, in_specs=(P("loop", "bulk"),),
        out_specs=P(None, "bulk", "loop"), check_vma=False)
```
